32 devices in a mesh: tm: 2 (over y), pairs: 16 (over z, x, core).
Axes of the slice: x: 2, y: 2, z: 4, core: 2. Of those that a mesh axis runs over, the one named last changes fastest.
Arguments:
- records: bfloat16 [2, 512, 128, 2048], P('tm', 'pairs')
- source_map: int32 [2, 512], P('tm'), may hold values from 0 to 511, each once within a row
- pair_blocks: int32 [16, 6, 2], P('pairs'), may hold values from -1 to 31, as said below
Outputs:
- stacks: float32 [96, 16, 2, 128, 128], P('pairs', 'tm')
The draws below stay inside these ranges and needn't reach their ends.
Inputs may be any that keep to these rules, and one draw needn't show every extreme that they name: `pair_blocks`: each pair slot holds blocks i <= j with j - i <= 2, or -1 and -1 when empty; every such pair appears in exactly one slot; some owner has all 6 slots filled. `source_map`: each row is a permutation: every slot of a time group holds exactly one window of one channel block.
All inputs are finite; a program needn't handle non-finite values.
Results may differ from the reference program's by a relative error of at most 0.0056.
Values may be sent and summed in bfloat16 or wider, within the bound.
A program may use at most 128 MiB of HBM per device.

```python
import math
import jax
import jax.numpy as jnp
import numpy as np
from jax import lax

CB = 128
NB = 32
L = 2048
BINS = 16
FIRST_BIN = 64
DMAX = 2
WIN = 16
GROUP_ITEMS = 512
PC = 6
N_TM = 2
N_PAIRS = 16


def draw_records(key, part):
    first_key, second_key = jax.random.split(key, 2)
    shape_full = (N_TM, WIN * NB, CB, L)
    gains = jnp.exp(jax.random.uniform(second_key, (N_TM, WIN * NB, CB, 1), jnp.float32, 0.0, math.log(10.0)))
    base = jax.random.normal(first_key, shape_full, jnp.float32)
    return (base * gains).astype(jnp.bfloat16)


def draw_pair_blocks(key, part):
    listed = np.array([[start_block, start_block + offset] for offset in range(DMAX + 1) for start_block in range(NB - offset)], dtype=np.int32)
    total_slots = N_PAIRS * PC
    order = jax.random.permutation(jax.random.fold_in(key, 7), total_slots)[:listed.shape[0]]
    table_rows = jnp.full((total_slots, 2), -1, jnp.int32).at[order].set(jnp.asarray(listed))
    return table_rows.reshape(N_PAIRS, PC, 2)


def setup_inputs(seed: int = 0) -> dict:
    arg_keys = jax.random.split(jax.random.key(seed), 4)
    return {
        "records": draw_records(jax.random.fold_in(arg_keys[3], 71), 0),
        "source_map": jax.vmap(lambda own: jax.random.permutation(own, GROUP_ITEMS))(jax.random.split(arg_keys[1], N_TM)).reshape((N_TM, GROUP_ITEMS)).astype(jnp.int32),
        "pair_blocks": draw_pair_blocks(jax.random.fold_in(arg_keys[3], 71), 0),
    }


def transform_table(length):
    samples = jnp.arange(length, dtype=jnp.int32)
    bin_index = FIRST_BIN + jnp.arange(BINS, dtype=jnp.int32)
    phases = samples[:, None] * bin_index[None, :] % length
    angles = 2.0 * math.pi / length * phases.astype(jnp.float32)
    taper = 0.5 - 0.5 * jnp.cos(2.0 * math.pi / length * samples.astype(jnp.float32))
    weight_col = (taper / math.sqrt(length))[:, None]
    return jnp.concatenate([jnp.cos(angles) * weight_col, -jnp.sin(angles) * weight_col], axis=1).astype(jnp.bfloat16)

def whiten_spectra(windows, table):
    transformed = jnp.einsum('scn,nk->skc', windows.astype(jnp.float32), table.astype(jnp.float32), precision=lax.Precision.HIGHEST)
    real_part = transformed[:, :BINS]
    imag_part = transformed[:, BINS:]
    power = lax.optimization_barrier(jnp.mean(real_part * real_part + imag_part * imag_part, axis=2, keepdims=True))
    inverse = 1.0 / jnp.sqrt(power + 1e-06)
    return (transformed * jnp.concatenate([inverse, inverse], axis=1)).astype(jnp.bfloat16)

def reference(records, source_map, pair_blocks):
    table = transform_table(records.shape[3])
    spectra_all = lax.map(lambda group_rows: whiten_spectra(group_rows, table), records)
    ordered = jax.vmap(lambda spec_group, index_row: spec_group[index_row])(spectra_all, source_map)
    windows_total = ordered.shape[0] * WIN
    arranged = ordered.reshape(windows_total, NB, 2, BINS, ordered.shape[3])
    flat_pairs = pair_blocks.reshape(-1, 2)

    def one_pair(pair_row):
        valid = (pair_row[0] >= 0).astype(jnp.float32)
        safe_row = jnp.maximum(pair_row, 0).astype(jnp.int32)
        left_spec = arranged[:, safe_row[0]].astype(jnp.float32)
        right_spec = arranged[:, safe_row[1]].astype(jnp.float32)
        real_sum = jnp.einsum('wfi,wfj->fij', left_spec[:, 0], right_spec[:, 0]) + jnp.einsum('wfi,wfj->fij', left_spec[:, 1], right_spec[:, 1])
        imag_sum = jnp.einsum('wfi,wfj->fij', left_spec[:, 1], right_spec[:, 0]) - jnp.einsum('wfi,wfj->fij', left_spec[:, 0], right_spec[:, 1])
        return jnp.stack([real_sum, imag_sum], axis=1) * (valid / math.sqrt(windows_total))
    return lax.map(one_pair, flat_pairs)
```

```python
import functools
import math

import jax
import jax.numpy as jnp
import numpy as np
from jax import lax
from jax.experimental import pallas as pl
from jax.experimental.pallas import tpu as pltpu
from jax.sharding import PartitionSpec as P

NB = 32
BINS = 16
FIRST_BIN = 64
WIN = 16
MESH = pl.DeviceIdType.MESH


def transform_table(length):
    samples = jnp.arange(length, dtype=jnp.int32)
    bin_index = FIRST_BIN + jnp.arange(BINS, dtype=jnp.int32)
    phases = samples[:, None] * bin_index[None, :] % length
    angles = 2.0 * math.pi / length * phases.astype(jnp.float32)
    taper = 0.5 - 0.5 * jnp.cos(2.0 * math.pi / length * samples.astype(jnp.float32))
    weight_col = (taper / math.sqrt(length))[:, None]
    return jnp.concatenate(
        [jnp.cos(angles) * weight_col, -jnp.sin(angles) * weight_col], axis=1
    ).astype(jnp.bfloat16)


def whiten_spectra(windows, table):
    transformed = jnp.einsum("scn,nk->skc", windows, table, preferred_element_type=jnp.float32)
    real_part = transformed[:, :BINS]
    imag_part = transformed[:, BINS:]
    power = jnp.mean(real_part * real_part + imag_part * imag_part, axis=2, keepdims=True)
    inverse = 1.0 / jnp.sqrt(power + 1e-06)
    return (transformed * jnp.concatenate([inverse, inverse], axis=1)).astype(jnp.bfloat16)


def exchange_kernel(groups, pairs, own_ref, map_ref, out_ref, maps_ref,
                    send_sems, recv_sems, tm_send, map_send, map_recv, local_sems):
    depth = pairs // 4
    t = lax.axis_index("tm")
    me = lax.axis_index("pairs")
    z = me // 4
    x = (me // 2) % 2
    c = me % 2

    def slot(zz, xx, cc):
        return zz * 4 + xx * 2 + cc

    up, down = me + 4, me - 4
    side = slot(z, 1 - x, c)
    twin = slot(z, x, 1 - c)
    has_up = z < depth - 1
    has_down = z > 0

    barrier = pltpu.get_barrier_semaphore()
    for d in range(1, groups):
        pl.semaphore_signal(barrier, inc=1, device_id=((t + d) % groups, me), device_id_type=MESH)
    for other in (side, twin):
        pl.semaphore_signal(barrier, inc=1, device_id=(t, other), device_id_type=MESH)

    @pl.when(has_up)
    def _():
        pl.semaphore_signal(barrier, inc=1, device_id=(t, up), device_id_type=MESH)

    @pl.when(has_down)
    def _():
        pl.semaphore_signal(barrier, inc=1, device_id=(t, down), device_id_type=MESH)

    pl.semaphore_wait(barrier, groups + 1 + has_up.astype(jnp.int32) + has_down.astype(jnp.int32))

    def send(way, group, place, target, source=None):
        piece = out_ref.at[group, place]
        return pltpu.make_async_remote_copy(
            src_ref=piece if source is None else source,
            dst_ref=piece,
            send_sem=send_sems.at[way, group, place],
            recv_sem=recv_sems.at[group, place],
            device_id=(t, target),
            device_id_type=MESH,
        )

    def arrived(group, place):
        pltpu.make_async_copy(
            out_ref.at[group, place], out_ref.at[group, place], recv_sems.at[group, place]
        ).wait()

    def tm_copy(d):
        peer = (t + d) % groups
        return pltpu.make_async_remote_copy(
            src_ref=own_ref.at[peer],
            dst_ref=out_ref.at[t, me],
            send_sem=tm_send.at[d],
            recv_sem=recv_sems.at[t, me],
            device_id=(peer, me),
            device_id_type=MESH,
        )

    def map_copy(d):
        peer = (t + d) % groups
        return pltpu.make_async_remote_copy(
            src_ref=map_ref.at[0],
            dst_ref=maps_ref.at[t],
            send_sem=map_send.at[d],
            recv_sem=map_recv.at[t],
            device_id=(peer, me),
            device_id_type=MESH,
        )

    for d in range(1, groups):
        tm_copy(d).start()
        map_copy(d).start()
    keep = pltpu.make_async_copy(own_ref.at[t], out_ref.at[t, me], local_sems.at[0])
    keep.start()
    keep_map = pltpu.make_async_copy(map_ref.at[0], maps_ref.at[t], local_sems.at[1])
    keep_map.start()

    def spread(group, place, source, upward, downward):
        if upward is not None:
            @pl.when(upward)
            def _():
                send(0, group, place, up, source).start()
        if downward is not None:
            @pl.when(downward)
            def _():
                send(1, group, place, down, source).start()
        send(2, group, place, side, source).start()
        send(3, group, place, twin, source).start()

    order = [(t + d) % groups for d in range(groups)]
    for d, group in enumerate(order):
        if d:
            arrived(group, me)
        spread(group, me, None if d else own_ref.at[t], has_up, has_down)

    def side_arrivals(step):
        for group in order:
            for sign in ((1, -1) if step else (0,)):
                where = z + sign * step

                @pl.when((where >= 0) & (where < depth))
                def _():
                    place = slot(where, 1 - x, c)
                    arrived(group, place)
                    send(3, group, place, twin).start()

    for step in range(1, depth):
        for group in order:
            @pl.when(z - step >= 0)
            def _():
                place = slot(z - step, x, c)
                arrived(group, place)
                spread(group, place, None, has_up, None)

            @pl.when(z + step < depth)
            def _():
                place = slot(z + step, x, c)
                arrived(group, place)
                spread(group, place, None, None, has_down)
        if step >= 2:
            side_arrivals(step - 2)
    for step in range(max(depth - 2, 0), depth):
        side_arrivals(step)

    keep.wait()
    keep_map.wait()
    for d in range(1, groups):
        tm_copy(d).wait_send()
        map_copy(d).wait_send()
        pltpu.make_async_copy(
            maps_ref.at[order[d]], maps_ref.at[order[d]], map_recv.at[order[d]]
        ).wait()
    for group in order:
        for zz in range(depth):
            for xx in range(2):
                arrived(group, slot(zz, xx, 1 - c))
    for group in order:
        for zz in range(depth):
            place = slot(zz, x, c)

            @pl.when(has_up & (zz <= z))
            def _():
                send(0, group, place, up).wait_send()

            @pl.when(has_down & (zz >= z))
            def _():
                send(1, group, place, down).wait_send()

            send(2, group, place, side).wait_send()
            send(3, group, place, twin).wait_send()
            send(3, group, slot(zz, 1 - x, c), twin).wait_send()


def exchange(own, local_map, groups, pairs):
    _, rows, width = own.shape
    return pl.pallas_call(
        functools.partial(exchange_kernel, groups, pairs),
        out_shape=(
            jax.ShapeDtypeStruct((groups, pairs, rows, width), own.dtype),
            jax.ShapeDtypeStruct((groups,) + local_map.shape[1:], local_map.dtype),
        ),
        in_specs=[pl.BlockSpec(memory_space=pl.ANY)] * 2,
        out_specs=(pl.BlockSpec(memory_space=pl.ANY),) * 2,
        scratch_shapes=[
            pltpu.SemaphoreType.DMA((4, groups, pairs)),
            pltpu.SemaphoreType.DMA((groups, pairs)),
            pltpu.SemaphoreType.DMA((groups,)),
            pltpu.SemaphoreType.DMA((groups,)),
            pltpu.SemaphoreType.DMA((groups,)),
            pltpu.SemaphoreType.DMA((2,)),
        ],
        compiler_params=pltpu.CompilerParams(collective_id=0, has_side_effects=True),
        name="exchange",
    )(own, local_map)


def stack_kernel(groups, slots, bins, channels, scale, blocks_ref, maps_ref, spectra_ref, out_ref, picked):
    s = pl.program_id(0)
    items = spectra_ref.shape[1]

    @pl.when(s == 0)
    def _():
        lanes = lax.broadcasted_iota(jnp.int32, (WIN, NB), 1)
        rows = lax.broadcasted_iota(jnp.int32, (WIN, items), 1)
        for group in range(groups):
            table = maps_ref[group]
            parts = []
            for ref in range(2 * slots):
                block = jnp.maximum(blocks_ref[ref], 0)
                source = jnp.sum(jnp.where(lanes == block, table, 0), axis=1, keepdims=True)
                parts.append((rows == source).astype(jnp.float32))
            onehot = jnp.concatenate(parts, axis=0).astype(jnp.bfloat16)
            picked[group] = jnp.dot(
                onehot, spectra_ref[group], preferred_element_type=jnp.float32
            ).astype(jnp.bfloat16)

    factor = jnp.where(blocks_ref[2 * s] >= 0, scale, 0.0).astype(jnp.float32)
    left = pl.ds(pl.multiple_of(s * 2 * WIN, 2 * WIN), WIN)
    right = pl.ds(pl.multiple_of(s * 2 * WIN + WIN, WIN), WIN)
    for f in range(bins):
        real = slice(f * channels, (f + 1) * channels)
        imag = slice((bins + f) * channels, (bins + f + 1) * channels)
        x_re = [picked[g, left, real] for g in range(groups)]
        x_im = [picked[g, left, imag] for g in range(groups)]
        y_re = jnp.concatenate([picked[g, right, real] for g in range(groups)], axis=0)
        y_im = jnp.concatenate([picked[g, right, imag] for g in range(groups)], axis=0)
        lhs = jnp.concatenate(x_re + x_im, axis=0)
        rhs = jnp.concatenate(
            [
                jnp.concatenate([y_re, -y_im], axis=1),
                jnp.concatenate([y_im, y_re], axis=1),
            ],
            axis=0,
        )
        both = lax.dot_general(lhs, rhs, (((0,), (0,)), ((), ())), preferred_element_type=jnp.float32)
        out_ref[0, f, 0] = both[:, :channels] * factor
        out_ref[0, f, 1] = both[:, channels:] * factor


def stack_pairs(blocks, maps, spectra, slots, channels):
    groups, items, width = spectra.shape
    bins = width // (2 * channels)
    scale = 1.0 / math.sqrt(WIN * groups)
    return pl.pallas_call(
        functools.partial(stack_kernel, groups, slots, bins, channels, scale),
        out_shape=jax.ShapeDtypeStruct((slots, bins, 2, channels, channels), jnp.float32),
        grid_spec=pltpu.PrefetchScalarGridSpec(
            num_scalar_prefetch=1,
            grid=(slots,),
            in_specs=[
                pl.BlockSpec((groups, WIN, NB), lambda s, b: (0, 0, 0)),
                pl.BlockSpec((groups, items, width), lambda s, b: (0, 0, 0), pipeline_mode=pl.Buffered(1)),
            ],
            out_specs=pl.BlockSpec((1, bins, 2, channels, channels), lambda s, b: (s, 0, 0, 0, 0)),
            scratch_shapes=[pltpu.VMEM((groups, 2 * slots * WIN, width), jnp.bfloat16)],
        ),
        compiler_params=pltpu.CompilerParams(
            dimension_semantics=("arbitrary",), vmem_limit_bytes=40 << 20
        ),
        name="stack_pairs",
    )(blocks, maps, spectra)


def per_device(groups, pairs, records, source_map, pair_blocks):
    table = transform_table(records.shape[3])
    local_spec = whiten_spectra(records[0], table)
    items, _, channels = local_spec.shape
    bins = BINS // groups
    own = local_spec.reshape(items, 2, groups, bins, channels)
    own = own.transpose(2, 0, 1, 3, 4).reshape(groups, items, 2 * bins * channels)
    gathered, maps = exchange(own, source_map.reshape(1, WIN, NB), groups, pairs)
    spectra = gathered.reshape(groups, pairs * items, 2 * bins * channels)
    slots = pair_blocks.shape[1]
    return stack_pairs(pair_blocks.reshape(-1), maps, spectra, slots, channels)


def solution(mesh):
    groups, pairs = mesh.shape["tm"], mesh.shape["pairs"]
    return jax.shard_map(
        functools.partial(per_device, groups, pairs),
        mesh=mesh,
        in_specs=(P("tm", "pairs", None, None), P("tm", None), P("pairs", None, None)),
        out_specs=P("pairs", "tm", None, None, None),
        check_vma=False,
    )
```

```python
import functools
import math

import jax
import jax.numpy as jnp
import numpy as np
from jax import lax
from jax.experimental import pallas as pl
from jax.experimental.pallas import tpu as pltpu
from jax.sharding import PartitionSpec as P

NB = 32
BINS = 16
FIRST_BIN = 64
WIN = 16
MESH = pl.DeviceIdType.MESH


def transform_table(length):
    samples = jnp.arange(length, dtype=jnp.int32)
    bin_index = FIRST_BIN + jnp.arange(BINS, dtype=jnp.int32)
    phases = samples[:, None] * bin_index[None, :] % length
    angles = 2.0 * math.pi / length * phases.astype(jnp.float32)
    taper = 0.5 - 0.5 * jnp.cos(2.0 * math.pi / length * samples.astype(jnp.float32))
    weight_col = (taper / math.sqrt(length))[:, None]
    return jnp.concatenate(
        [jnp.cos(angles) * weight_col, -jnp.sin(angles) * weight_col], axis=1
    ).astype(jnp.bfloat16)


def gather_kernel(groups, pairs, blocks_ref, map_ref, table_ref, records_ref, picked_ref,
                  stream, raw, own, spectra, maps, onehot,
                  load_sems, send_sems, recv_sems, tm_send, map_send, map_recv, keep_sems):
    items, channels, _ = records_ref.shape
    pieces, rows, width = own.shape[1:]
    batch = stream.shape[1]
    bins = width // (2 * channels)
    slots = blocks_ref.shape[1]
    depth = pairs // 4
    layer = 4 * items
    t = lax.axis_index("tm")
    me = lax.axis_index("pairs")
    z = me // 4
    x = (me // 2) % 2
    c = me % 2

    def slot(zz, xx, cc):
        return zz * 4 + xx * 2 + cc

    up, down = me + 4, me - 4
    side = slot(z, 1 - x, c)
    twin = slot(z, x, 1 - c)
    has_up = z < depth - 1
    has_down = z > 0
    batches = items // batch
    depth_in = stream.shape[0]

    def load(i):
        return pltpu.make_async_copy(
            records_ref.at[pl.ds(i * batch, batch)], stream.at[i % depth_in], load_sems.at[i % depth_in]
        )

    for i in range(min(depth_in, batches)):
        load(i).start()

    barrier = pltpu.get_barrier_semaphore()
    for d in range(1, groups):
        pl.semaphore_signal(barrier, inc=1, device_id=((t + d) % groups, me), device_id_type=MESH)
    for other in (side, twin):
        pl.semaphore_signal(barrier, inc=1, device_id=(t, other), device_id_type=MESH)

    @pl.when(has_up)
    def _():
        pl.semaphore_signal(barrier, inc=1, device_id=(t, up), device_id_type=MESH)

    @pl.when(has_down)
    def _():
        pl.semaphore_signal(barrier, inc=1, device_id=(t, down), device_id_type=MESH)

    def send(way, group, place, target, source=None):
        piece = spectra.at[group, place]
        return pltpu.make_async_remote_copy(
            src_ref=piece if source is None else source,
            dst_ref=piece,
            send_sem=send_sems.at[way, group, place],
            recv_sem=recv_sems.at[group, place],
            device_id=(t, target),
            device_id_type=MESH,
        )

    def arrived(group, place):
        pltpu.make_async_copy(
            spectra.at[group, place], spectra.at[group, place], recv_sems.at[group, place]
        ).wait()

    def tm_copy(d, k):
        peer = (t + d) % groups
        place = me * pieces + k
        return pltpu.make_async_remote_copy(
            src_ref=own.at[peer, k],
            dst_ref=spectra.at[t, place],
            send_sem=tm_send.at[d, k],
            recv_sem=recv_sems.at[t, place],
            device_id=(peer, me),
            device_id_type=MESH,
        )

    def map_copy(d):
        peer = (t + d) % groups
        return pltpu.make_async_remote_copy(
            src_ref=map_ref,
            dst_ref=maps.at[t],
            send_sem=map_send.at[d],
            recv_sem=map_recv.at[t],
            device_id=(peer, me),
            device_id_type=MESH,
        )

    def keep(k):
        return pltpu.make_async_copy(own.at[t, k], spectra.at[t, me * pieces + k], keep_sems.at[k])

    def spread(group, place, source, upward, downward):
        if upward is not None:
            @pl.when(upward)
            def _():
                send(0, group, place, up, source).start()
        if downward is not None:
            @pl.when(downward)
            def _():
                send(1, group, place, down, source).start()
        send(2, group, place, side, source).start()
        send(3, group, place, twin, source).start()

    order = [(t + d) % groups for d in range(groups)]

    for k in range(pieces):
        for j in range(rows // batch):
            i = k * (rows // batch) + j
            load(i).wait()
            block = stream[i % depth_in].reshape(batch * channels, records_ref.shape[2])
            both = lax.dot_general(
                table_ref[...], block, (((1,), (1,)), ((), ())), preferred_element_type=jnp.float32
            )
            if i + depth_in < batches:
                load(i + depth_in).start()
            for r in range(batch):
                real = both[:BINS, r * channels:(r + 1) * channels]
                imag = both[BINS:, r * channels:(r + 1) * channels]
                power = jnp.mean(real * real + imag * imag, axis=1, keepdims=True)
                inverse = 1.0 / jnp.sqrt(power + 1e-06)
                raw[j * batch + r, :BINS] = real * inverse
                raw[j * batch + r, BINS:] = imag * inverse
        turned = jnp.transpose(raw[...], (1, 0, 2)).astype(jnp.bfloat16)
        for h in range(groups):
            for part in range(2):
                for f in range(bins):
                    col = (part * bins + f) * channels
                    own[h, k, :, col:col + channels] = turned[part * BINS + h * bins + f]
        if k == 0:
            pl.semaphore_wait(
                barrier, groups + 1 + has_up.astype(jnp.int32) + has_down.astype(jnp.int32)
            )
            for d in range(1, groups):
                map_copy(d).start()
        spread(t, me * pieces + k, own.at[t, k], has_up, has_down)
        for d in range(1, groups):
            tm_copy(d, k).start()
        keep(k).start()

    maps[t] = map_ref[...]
    for k in range(pieces):
        for group in order[1:]:
            arrived(group, me * pieces + k)
            spread(group, me * pieces + k, None, has_up, has_down)

    total = maps.shape[2]
    wanted_lane = lax.broadcasted_iota(jnp.int32, (WIN, total), 0) * NB
    lane = lax.broadcasted_iota(jnp.int32, (WIN, total), 1)
    column = lax.broadcasted_iota(jnp.int32, (WIN, layer), 1)
    for d, group in enumerate(order):
        if d:
            pltpu.make_async_copy(maps.at[group], maps.at[group], map_recv.at[group]).wait()
        table = jnp.broadcast_to(maps[group], (WIN, total))
        for ref in range(2 * slots):
            block = jnp.maximum(blocks_ref[0, ref // 2, ref % 2], 0)
            source = jnp.sum(
                jnp.where(lane == wanted_lane + block, table, 0), axis=1, keepdims=True
            )
            for zz in range(depth):
                hit = (column + zz * layer == source).astype(jnp.float32).astype(jnp.bfloat16)
                onehot[group, zz, ref * WIN:(ref + 1) * WIN, :] = hit
    picked_ref[...] = jnp.zeros_like(picked_ref)
    for k in range(pieces):
        keep(k).wait()

    def pick(zz):
        for group in order:
            for xx in range(2):
                for k in range(pieces):
                    arrived(group, slot(zz, xx, 1 - c) * pieces + k)

        @pl.loop(0, groups)
        def _(group):
            rows_in = spectra[group, pl.ds(zz * 4 * pieces, 4 * pieces)].reshape(layer, width)
            found = jnp.dot(onehot[group, zz], rows_in, preferred_element_type=jnp.float32)
            picked_ref[group] += found.astype(jnp.bfloat16)

    @pl.loop(1, depth + 2)
    def _(step):
        for k in range(pieces):
            for group in order:
                @pl.when(z - step >= 0)
                def _():
                    place = slot(z - step, x, c) * pieces + k
                    arrived(group, place)
                    spread(group, place, None, has_up, None)

                @pl.when(z + step < depth)
                def _():
                    place = slot(z + step, x, c) * pieces + k
                    arrived(group, place)
                    spread(group, place, None, None, has_down)

        for k in range(pieces):
            for group in order:
                for sign in (1, -1):
                    where = z + sign * (step - 1)
                    there = (where >= 0) & (where < depth)

                    @pl.when(there if sign == 1 else there & (step > 1))
                    def _():
                        place = slot(where, 1 - x, c) * pieces + k
                        arrived(group, place)
                        send(3, group, place, twin).start()

        for sign in (1, -1):
            where = z + sign * (step - 2)
            there = (where >= 0) & (where < depth)

            @pl.when(there & (step > (1 if sign == 1 else 2)))
            def _():
                pick(where)

    for d in range(1, groups):
        map_copy(d).wait_send()
        for k in range(pieces):
            tm_copy(d, k).wait_send()

    @pl.loop(0, depth)
    def _(zz):
        for k in range(pieces):
            for group in order:
                place = slot(zz, x, c) * pieces + k

                @pl.when(has_up & (zz <= z))
                def _():
                    send(0, group, place, up).wait_send()

                @pl.when(has_down & (zz >= z))
                def _():
                    send(1, group, place, down).wait_send()

                send(2, group, place, side).wait_send()
                send(3, group, place, twin).wait_send()
                send(3, group, slot(zz, 1 - x, c) * pieces + k, twin).wait_send()


def gather_picked(pair_blocks, source_map, table, records, groups, pairs):
    items, channels, length = records.shape
    slots = pair_blocks.shape[1]
    width = 2 * (BINS // groups) * channels
    rows = min(16, items)
    pieces = items // rows
    batch = min(4, rows)
    dtype = jnp.bfloat16
    vmem = pl.BlockSpec(memory_space=pltpu.VMEM)
    return pl.pallas_call(
        functools.partial(gather_kernel, groups, pairs),
        out_shape=jax.ShapeDtypeStruct((groups, 2 * slots * WIN, width), dtype),
        in_specs=[
            pl.BlockSpec(memory_space=pltpu.SMEM),
            vmem,
            vmem,
            pl.BlockSpec(memory_space=pl.ANY),
        ],
        out_specs=vmem,
        scratch_shapes=[
            pltpu.VMEM((3, batch, channels, length), dtype),
            pltpu.VMEM((rows, 2 * BINS, channels), jnp.float32),
            pltpu.VMEM((groups, pieces, rows, width), dtype),
            pltpu.VMEM((groups, pairs * pieces, rows, width), dtype),
            pltpu.VMEM((groups,) + source_map.shape, jnp.int32),
            pltpu.VMEM((groups, pairs // 4, 2 * slots * WIN, 4 * items), dtype),
            pltpu.SemaphoreType.DMA((3,)),
            pltpu.SemaphoreType.DMA((4, groups, pairs * pieces)),
            pltpu.SemaphoreType.DMA((groups, pairs * pieces)),
            pltpu.SemaphoreType.DMA((groups, pieces)),
            pltpu.SemaphoreType.DMA((groups,)),
            pltpu.SemaphoreType.DMA((groups,)),
            pltpu.SemaphoreType.DMA((pieces,)),
        ],
        compiler_params=pltpu.CompilerParams(
            collective_id=0, has_side_effects=True, vmem_limit_bytes=40 << 20
        ),
        name="gather_picked",
    )(pair_blocks, source_map, table, records)


def stack_kernel(groups, bins, channels, scale, blocks_ref, picked_ref, out_ref):
    s = pl.program_id(0)
    factor = jnp.where(blocks_ref[0, s, 0] >= 0, scale, 0.0).astype(jnp.float32)
    for f in range(bins):
        real = slice(f * channels, (f + 1) * channels)
        imag = slice((bins + f) * channels, (bins + f + 1) * channels)
        x_re = [picked_ref[g, :WIN, real] for g in range(groups)]
        x_im = [picked_ref[g, :WIN, imag] for g in range(groups)]
        y_re = jnp.concatenate([picked_ref[g, WIN:, real] for g in range(groups)], axis=0)
        y_im = jnp.concatenate([picked_ref[g, WIN:, imag] for g in range(groups)], axis=0)
        lhs = jnp.concatenate(x_re + x_im, axis=0)
        rhs = jnp.concatenate(
            [
                jnp.concatenate([y_re, -y_im], axis=1),
                jnp.concatenate([y_im, y_re], axis=1),
            ],
            axis=0,
        )
        both = lax.dot_general(lhs, rhs, (((0,), (0,)), ((), ())), preferred_element_type=jnp.float32)
        out_ref[0, f, 0] = both[:, :channels] * factor
        out_ref[0, f, 1] = both[:, channels:] * factor


def stack_pairs(pair_blocks, picked, channels):
    groups, _, width = picked.shape
    slots = pair_blocks.shape[1]
    bins = width // (2 * channels)
    scale = 1.0 / math.sqrt(WIN * groups)
    return pl.pallas_call(
        functools.partial(stack_kernel, groups, bins, channels, scale),
        out_shape=jax.ShapeDtypeStruct((slots, bins, 2, channels, channels), jnp.float32),
        grid=(slots,),
        in_specs=[
            pl.BlockSpec(memory_space=pltpu.SMEM),
            pl.BlockSpec((groups, 2 * WIN, width), lambda s: (0, s, 0)),
        ],
        out_specs=pl.BlockSpec((1, bins, 2, channels, channels), lambda s: (s, 0, 0, 0, 0)),
        compiler_params=pltpu.CompilerParams(
            dimension_semantics=("arbitrary",), vmem_limit_bytes=40 << 20
        ),
        name="stack_pairs",
    )(pair_blocks, picked)


def per_device(groups, pairs, records, source_map, pair_blocks):
    table = transform_table(records.shape[3]).T
    picked = gather_picked(pair_blocks, source_map, table, records[0], groups, pairs)
    return stack_pairs(pair_blocks, picked, records.shape[2])


def solution(mesh):
    groups, pairs = mesh.shape["tm"], mesh.shape["pairs"]
    return jax.shard_map(
        functools.partial(per_device, groups, pairs),
        mesh=mesh,
        in_specs=(P("tm", "pairs", None, None), P("tm", None), P("pairs", None, None)),
        out_specs=P("pairs", "tm", None, None, None),
        check_vma=False,
    )
```

```python
import functools
import math

import jax
import jax.numpy as jnp
import numpy as np
from jax import lax
from jax.experimental import pallas as pl
from jax.experimental.pallas import tpu as pltpu
from jax.sharding import PartitionSpec as P

NB = 32
BINS = 16
FIRST_BIN = 64
WIN = 16
MESH = pl.DeviceIdType.MESH


def transform_table(length):
    samples = np.arange(length)
    phases = samples[None, :] * (FIRST_BIN + np.arange(BINS))[:, None] % length
    angles = 2.0 * np.pi / length * phases
    weight = (0.5 - 0.5 * np.cos(2.0 * np.pi / length * samples)) / math.sqrt(length)
    rows = np.concatenate([np.cos(angles) * weight, -np.sin(angles) * weight])
    return rows.astype(np.float32).astype(jnp.bfloat16)


def gather_kernel(groups, pairs, blocks_ref, map_ref, table_ref, records_ref, picked_ref,
                  table, stream, raw, own, spectra, maps, onehot,
                  table_sem, load_sems, send_sems, recv_sems, tm_send, map_send, map_recv, keep_sems):
    items, channels, _ = records_ref.shape
    pieces, rows, width = own.shape[1:]
    batch = stream.shape[1]
    bins = width // (2 * channels)
    slots = blocks_ref.shape[1]
    depth = pairs // 4
    layer = 4 * items
    t = lax.axis_index("tm")
    me = lax.axis_index("pairs")
    z = me // 4
    x = (me // 2) % 2
    c = me % 2

    def slot(zz, xx, cc):
        return zz * 4 + xx * 2 + cc

    up, down = me + 4, me - 4
    side = slot(z, 1 - x, c)
    twin = slot(z, x, 1 - c)
    has_up = z < depth - 1
    has_down = z > 0
    batches = items // batch
    depth_in = stream.shape[0]

    def load(i):
        return pltpu.make_async_copy(
            records_ref.at[pl.ds(i * batch, batch)], stream.at[i % depth_in], load_sems.at[i % depth_in]
        )

    fetch_table = pltpu.make_async_copy(table_ref, table, table_sem.at[0])
    fetch_table.start()
    for i in range(min(depth_in, batches)):
        load(i).start()

    barrier = pltpu.get_barrier_semaphore()
    for d in range(1, groups):
        pl.semaphore_signal(barrier, inc=1, device_id=((t + d) % groups, me), device_id_type=MESH)
    for other in (side, twin):
        pl.semaphore_signal(barrier, inc=1, device_id=(t, other), device_id_type=MESH)

    @pl.when(has_up)
    def _():
        pl.semaphore_signal(barrier, inc=1, device_id=(t, up), device_id_type=MESH)

    @pl.when(has_down)
    def _():
        pl.semaphore_signal(barrier, inc=1, device_id=(t, down), device_id_type=MESH)

    def send(way, group, place, target, source=None):
        piece = spectra.at[group, place]
        return pltpu.make_async_remote_copy(
            src_ref=piece if source is None else source,
            dst_ref=piece,
            send_sem=send_sems.at[way, group, place],
            recv_sem=recv_sems.at[group, place],
            device_id=(t, target),
            device_id_type=MESH,
        )

    def arrived(group, place):
        pltpu.make_async_copy(
            spectra.at[group, place], spectra.at[group, place], recv_sems.at[group, place]
        ).wait()

    def tm_copy(d, k):
        peer = (t + d) % groups
        place = me * pieces + k
        return pltpu.make_async_remote_copy(
            src_ref=own.at[peer, k],
            dst_ref=spectra.at[t, place],
            send_sem=tm_send.at[d, k],
            recv_sem=recv_sems.at[t, place],
            device_id=(peer, me),
            device_id_type=MESH,
        )

    def map_copy(d):
        peer = (t + d) % groups
        return pltpu.make_async_remote_copy(
            src_ref=map_ref,
            dst_ref=maps.at[t],
            send_sem=map_send.at[d],
            recv_sem=map_recv.at[t],
            device_id=(peer, me),
            device_id_type=MESH,
        )

    def keep(k):
        return pltpu.make_async_copy(own.at[t, k], spectra.at[t, me * pieces + k], keep_sems.at[k])

    def over_line(where, k):
        half = k % 2 == 1
        below = (where == z - 1) & ((where == 0) | ((where == depth - 2) & half))
        above = (where == z + 1) & ((where == depth - 1) | ((where == 1) & half))
        return below | above

    def when_sent(condition, way, group, place, target, source=None):
        @pl.when(condition)
        def _():
            send(way, group, place, target, source).start()

    def first_spread(group, k, source=None):
        place = me * pieces + k
        send(2, group, place, side, source).start()
        when_sent(has_up, 0, group, place, up, source)
        when_sent(has_down, 1, group, place, down, source)
        send(3, group, place, twin, source).start()

    def column_arrival(step, group, k):
        for sign, onward, way, target in ((-1, has_up, 0, up), (1, has_down, 1, down)):
            where = z + sign * step

            @pl.when((where >= 0) & (where < depth))
            def _():
                place = slot(where, x, c) * pieces + k
                arrived(group, place)
                when_sent(onward, way, group, place, target)
                when_sent(jnp.logical_not(over_line(where, k)), 2, group, place, side)
                send(3, group, place, twin).start()

    def lift(k):
        return (z == 0) | ((z == depth - 2) & (k % 2 == 1))

    def lower(k):
        return (z == depth - 1) | ((z == 1) & (k % 2 == 1))

    def side_arrival(step, group, k):
        if isinstance(step, int):
            place = side * pieces + k
            arrived(group, place)
            when_sent(lift(k), 0, group, place, up)
            when_sent(lower(k), 1, group, place, down)
            send(3, group, place, twin).start()
            return
        for sign in (-1, 1):
            where = z + sign * step

            @pl.when((where >= 0) & (where < depth))
            def _():
                place = slot(where, 1 - x, c) * pieces + k
                arrived(group, place)
                send(3, group, place, twin).start()

    order = [(t + d) % groups for d in range(groups)]

    def early(j):
        if j == 1:
            for group in order[1:]:
                arrived(group, me * pieces)
                first_spread(group, 0)
        if j == 2:
            column_arrival(1, order[0], 0)
        if j == 3:
            side_arrival(0, order[0], 0)
            for group in order[1:]:
                column_arrival(1, group, 0)

    fetch_table.wait()
    for k in range(pieces):
        for j in range(rows // batch):
            i = k * (rows // batch) + j
            load(i).wait()
            block = stream[i % depth_in].reshape(batch * channels, records_ref.shape[2])
            both = lax.dot_general(
                table[...], block, (((1,), (1,)), ((), ())), preferred_element_type=jnp.float32
            )
            if i + depth_in < batches:
                load(i + depth_in).start()
            if k == 1:
                early(j)
            for r in range(batch):
                real = both[:BINS, r * channels:(r + 1) * channels]
                imag = both[BINS:, r * channels:(r + 1) * channels]
                power = jnp.mean(real * real + imag * imag, axis=1, keepdims=True)
                inverse = 1.0 / jnp.sqrt(power + 1e-06)
                raw[j * batch + r, :BINS] = real * inverse
                raw[j * batch + r, BINS:] = imag * inverse
        turned = jnp.transpose(raw[...], (1, 0, 2)).astype(jnp.bfloat16)
        for h in range(groups):
            for part in range(2):
                for f in range(bins):
                    col = (part * bins + f) * channels
                    own[h, k, :, col:col + channels] = turned[part * BINS + h * bins + f]
        if k == 0:
            pl.semaphore_wait(
                barrier, groups + 1 + has_up.astype(jnp.int32) + has_down.astype(jnp.int32)
            )
            for d in range(1, groups):
                map_copy(d).start()
        for d in range(1, groups):
            tm_copy(d, k).start()
        first_spread(t, k, own.at[t, k])
        keep(k).start()

    maps[t] = map_ref[...]
    split = pieces > 1
    for k in range(1 if split else 0, pieces):
        for group in order[1:]:
            arrived(group, me * pieces + k)
            first_spread(group, k)
    for k in range(1 if split else 0, pieces):
        for group in order:
            column_arrival(1, group, k)
    for k in range(pieces):
        for group in order:
            if not (split and k == 0) or group is not order[0]:
                side_arrival(0, group, k)

    total = maps.shape[2]
    wanted_lane = lax.broadcasted_iota(jnp.int32, (WIN, total), 0) * NB
    lane = lax.broadcasted_iota(jnp.int32, (WIN, total), 1)
    column = lax.broadcasted_iota(jnp.int32, (WIN, layer), 1)
    for d, group in enumerate(order):
        if d:
            pltpu.make_async_copy(maps.at[group], maps.at[group], map_recv.at[group]).wait()
        table = jnp.broadcast_to(maps[group], (WIN, total))
        for ref in range(2 * slots):
            block = jnp.maximum(blocks_ref[0, ref // 2:ref // 2 + 1, ref % 2:ref % 2 + 1], 0)
            source = jnp.sum(
                jnp.where(lane == wanted_lane + block, table, 0), axis=1, keepdims=True
            )
            for zz in range(depth):
                hit = (column + zz * layer == source).astype(jnp.float32).astype(jnp.bfloat16)
                onehot[group, zz, ref * WIN:(ref + 1) * WIN, :] = hit
    picked_ref[...] = jnp.zeros_like(picked_ref)
    for k in range(pieces):
        keep(k).wait()

    def pick(zz):
        for group in order:
            for xx in range(2):
                for k in range(pieces):
                    arrived(group, slot(zz, xx, 1 - c) * pieces + k)

        @pl.loop(0, groups)
        def _(group):
            rows_in = spectra[group, pl.ds(zz * 4 * pieces, 4 * pieces)].reshape(layer, width)
            found = jnp.dot(onehot[group, zz], rows_in, preferred_element_type=jnp.float32)
            picked_ref[group] += found.astype(jnp.bfloat16)

    @pl.loop(2, depth + 2)
    def _(step):
        for k in range(pieces):
            for group in order:
                column_arrival(step, group, k)
        for k in range(pieces):
            for group in order:
                side_arrival(step - 1, group, k)

        for sign in (1, -1):
            where = z + sign * (step - 2)
            there = (where >= 0) & (where < depth)

            @pl.when(there & (step > (1 if sign == 1 else 2)))
            def _():
                pick(where)

    for d in range(1, groups):
        map_copy(d).wait_send()
        for k in range(pieces):
            tm_copy(d, k).wait_send()

    for k in range(pieces):
        for group in order:
            @pl.when(lift(k))
            def _():
                send(0, group, side * pieces + k, up).wait_send()

            @pl.when(lower(k))
            def _():
                send(1, group, side * pieces + k, down).wait_send()

    @pl.loop(0, depth)
    def _(zz):
        for k in range(pieces):
            for group in order:
                place = slot(zz, x, c) * pieces + k

                @pl.when(has_up & (zz <= z))
                def _():
                    send(0, group, place, up).wait_send()

                @pl.when(has_down & (zz >= z))
                def _():
                    send(1, group, place, down).wait_send()

                @pl.when(jnp.logical_not(over_line(zz, k)))
                def _():
                    send(2, group, place, side).wait_send()

                send(3, group, place, twin).wait_send()
                send(3, group, slot(zz, 1 - x, c) * pieces + k, twin).wait_send()


def gather_picked(pair_blocks, source_map, table, records, groups, pairs):
    items, channels, length = records.shape
    slots = pair_blocks.shape[1]
    width = 2 * (BINS // groups) * channels
    rows = min(16, items)
    pieces = items // rows
    batch = min(4, rows)
    dtype = jnp.bfloat16
    vmem = pl.BlockSpec(memory_space=pltpu.VMEM)
    return pl.pallas_call(
        functools.partial(gather_kernel, groups, pairs),
        out_shape=jax.ShapeDtypeStruct((groups, 2 * slots * WIN, width), dtype),
        in_specs=[
            vmem,
            vmem,
            pl.BlockSpec(memory_space=pl.ANY),
            pl.BlockSpec(memory_space=pl.ANY),
        ],
        out_specs=vmem,
        scratch_shapes=[
            pltpu.VMEM((2 * BINS, length), dtype),
            pltpu.VMEM((3, batch, channels, length), dtype),
            pltpu.VMEM((rows, 2 * BINS, channels), jnp.float32),
            pltpu.VMEM((groups, pieces, rows, width), dtype),
            pltpu.VMEM((groups, pairs * pieces, rows, width), dtype),
            pltpu.VMEM((groups,) + source_map.shape, jnp.int32),
            pltpu.VMEM((groups, pairs // 4, 2 * slots * WIN, 4 * items), dtype),
            pltpu.SemaphoreType.DMA((1,)),
            pltpu.SemaphoreType.DMA((3,)),
            pltpu.SemaphoreType.DMA((4, groups, pairs * pieces)),
            pltpu.SemaphoreType.DMA((groups, pairs * pieces)),
            pltpu.SemaphoreType.DMA((groups, pieces)),
            pltpu.SemaphoreType.DMA((groups,)),
            pltpu.SemaphoreType.DMA((groups,)),
            pltpu.SemaphoreType.DMA((pieces,)),
        ],
        compiler_params=pltpu.CompilerParams(
            collective_id=0, has_side_effects=True, vmem_limit_bytes=40 << 20
        ),
        name="gather_picked",
    )(pair_blocks, source_map, table, records)


def stack_kernel(groups, scale, blocks_ref, picked_ref, out_ref, done, sems):
    slots, bins, _, channels, _ = out_ref.shape

    def write(s, f):
        return pltpu.make_async_copy(done.at[s, f], out_ref.at[s, f], sems.at[s, f])

    for s in range(slots):
        factor = jnp.where(blocks_ref[0, s:s + 1, 0:1] >= 0, scale, 0.0).astype(jnp.float32)
        factor = jnp.broadcast_to(factor, (channels, channels))
        left = slice(2 * s * WIN, (2 * s + 1) * WIN)
        right = slice((2 * s + 1) * WIN, (2 * s + 2) * WIN)
        for f in range(bins):
            real = slice(f * channels, (f + 1) * channels)
            imag = slice((bins + f) * channels, (bins + f + 1) * channels)
            x_re = [picked_ref[g, left, real] for g in range(groups)]
            x_im = [picked_ref[g, left, imag] for g in range(groups)]
            y_re = jnp.concatenate([picked_ref[g, right, real] for g in range(groups)], axis=0)
            y_im = jnp.concatenate([picked_ref[g, right, imag] for g in range(groups)], axis=0)
            lhs = jnp.concatenate(x_re + x_im, axis=0)
            rhs = jnp.concatenate(
                [
                    jnp.concatenate([y_re, -y_im], axis=1),
                    jnp.concatenate([y_im, y_re], axis=1),
                ],
                axis=0,
            )
            both = lax.dot_general(
                lhs, rhs, (((0,), (0,)), ((), ())), preferred_element_type=jnp.float32
            )
            done[s, f, 0] = both[:, :channels] * factor
            done[s, f, 1] = both[:, channels:] * factor
            write(s, f).start()
    for s in range(slots):
        for f in range(bins):
            write(s, f).wait()


def stack_pairs(pair_blocks, picked, channels):
    groups, _, width = picked.shape
    slots = pair_blocks.shape[1]
    bins = width // (2 * channels)
    scale = 1.0 / math.sqrt(WIN * groups)
    vmem = pl.BlockSpec(memory_space=pltpu.VMEM)
    shape = (slots, bins, 2, channels, channels)
    return pl.pallas_call(
        functools.partial(stack_kernel, groups, scale),
        out_shape=jax.ShapeDtypeStruct(shape, jnp.float32),
        in_specs=[vmem, vmem],
        out_specs=pl.BlockSpec(memory_space=pl.ANY),
        scratch_shapes=[pltpu.VMEM(shape, jnp.float32), pltpu.SemaphoreType.DMA((slots, bins))],
        compiler_params=pltpu.CompilerParams(vmem_limit_bytes=40 << 20),
        name="stack_pairs",
    )(pair_blocks, picked)


def per_device(groups, pairs, records, source_map, pair_blocks):
    table = jnp.asarray(transform_table(records.shape[3]))
    picked = gather_picked(pair_blocks, source_map, table, records[0], groups, pairs)
    return stack_pairs(pair_blocks, picked, records.shape[2])


def solution(mesh):
    groups, pairs = mesh.shape["tm"], mesh.shape["pairs"]
    return jax.shard_map(
        functools.partial(per_device, groups, pairs),
        mesh=mesh,
        in_specs=(P("tm", "pairs", None, None), P("tm", None), P("pairs", None, None)),
        out_specs=P("pairs", "tm", None, None, None),
        check_vma=False,
    )
```

```python
import functools
import math

import jax
import jax.numpy as jnp
import numpy as np
from jax import lax
from jax.experimental import pallas as pl
from jax.experimental.pallas import tpu as pltpu
from jax.sharding import PartitionSpec as P

NB = 32
BINS = 16
FIRST_BIN = 64
WIN = 16
MESH = pl.DeviceIdType.MESH


def transform_table(length):
    samples = np.arange(length)
    phases = samples[None, :] * (FIRST_BIN + np.arange(BINS))[:, None] % length
    angles = 2.0 * np.pi / length * phases
    weight = (0.5 - 0.5 * np.cos(2.0 * np.pi / length * samples)) / math.sqrt(length)
    rows = np.concatenate([np.cos(angles) * weight, -np.sin(angles) * weight])
    return rows.astype(np.float32).astype(jnp.bfloat16)


def gather_kernel(groups, pairs, blocks_ref, map_ref, table_ref, records_ref, picked_ref,
                  table, blocks, stream, raw, own, spectra, maps, onehot,
                  small_sems, load_sems, send_sems, recv_sems, tm_send, map_send, map_recv, keep_sems):
    items, channels, _ = records_ref.shape
    pieces, rows, width = own.shape[1:]
    batch = stream.shape[1]
    bins = width // (2 * channels)
    slots = blocks.shape[2]
    depth = pairs // 4
    layer = 4 * items
    t = lax.axis_index("tm")
    me = lax.axis_index("pairs")
    z = me // 4
    x = (me // 2) % 2
    c = me % 2

    def slot(zz, xx, cc):
        return zz * 4 + xx * 2 + cc

    up, down = me + 4, me - 4
    side = slot(z, 1 - x, c)
    twin = slot(z, x, 1 - c)
    has_up = z < depth - 1
    has_down = z > 0
    batches = items // batch
    depth_in = stream.shape[0]

    def load(i):
        return pltpu.make_async_copy(
            records_ref.at[pl.ds(i * batch, batch)], stream.at[i % depth_in], load_sems.at[i % depth_in]
        )

    fetch_table = pltpu.make_async_copy(table_ref, table, small_sems.at[0])
    fetch_table.start()
    fetch_blocks = pltpu.make_async_copy(blocks_ref, blocks, small_sems.at[1])
    fetch_blocks.start()
    keep_map = pltpu.make_async_copy(map_ref, maps.at[t], small_sems.at[2])
    keep_map.start()
    for i in range(min(depth_in, batches)):
        load(i).start()

    barrier = pltpu.get_barrier_semaphore()
    for d in range(1, groups):
        pl.semaphore_signal(barrier, inc=1, device_id=((t + d) % groups, me), device_id_type=MESH)
    for other in (side, twin):
        pl.semaphore_signal(barrier, inc=1, device_id=(t, other), device_id_type=MESH)

    @pl.when(has_up)
    def _():
        pl.semaphore_signal(barrier, inc=1, device_id=(t, up), device_id_type=MESH)

    @pl.when(has_down)
    def _():
        pl.semaphore_signal(barrier, inc=1, device_id=(t, down), device_id_type=MESH)

    def send(way, group, place, target, source=None):
        piece = spectra.at[group, place]
        return pltpu.make_async_remote_copy(
            src_ref=piece if source is None else source,
            dst_ref=piece,
            send_sem=send_sems.at[way, group, place],
            recv_sem=recv_sems.at[group, place],
            device_id=(t, target),
            device_id_type=MESH,
        )

    def arrived(group, place):
        pltpu.make_async_copy(
            spectra.at[group, place], spectra.at[group, place], recv_sems.at[group, place]
        ).wait()

    def tm_copy(d, k):
        peer = (t + d) % groups
        place = me * pieces + k
        return pltpu.make_async_remote_copy(
            src_ref=own.at[peer, k],
            dst_ref=spectra.at[t, place],
            send_sem=tm_send.at[d, k],
            recv_sem=recv_sems.at[t, place],
            device_id=(peer, me),
            device_id_type=MESH,
        )

    def map_copy(d):
        peer = (t + d) % groups
        return pltpu.make_async_remote_copy(
            src_ref=map_ref,
            dst_ref=maps.at[t],
            send_sem=map_send.at[d],
            recv_sem=map_recv.at[t],
            device_id=(peer, me),
            device_id_type=MESH,
        )

    def keep(k):
        return pltpu.make_async_copy(own.at[t, k], spectra.at[t, me * pieces + k], keep_sems.at[k])

    def over_line(where):
        return ((where == z - 1) & (where == 0)) | ((where == z + 1) & (where == depth - 1))

    def when_sent(condition, way, group, place, target, source=None):
        @pl.when(condition)
        def _():
            send(way, group, place, target, source).start()

    def first_spread(group, k, source=None):
        place = me * pieces + k
        send(2, group, place, side, source).start()
        when_sent(has_up, 0, group, place, up, source)
        when_sent(has_down, 1, group, place, down, source)
        send(3, group, place, twin, source).start()

    def column_arrival(step, group, k):
        for sign, onward, way, target in ((-1, has_up, 0, up), (1, has_down, 1, down)):
            where = z + sign * step

            @pl.when((where >= 0) & (where < depth))
            def _():
                place = slot(where, x, c) * pieces + k
                arrived(group, place)
                when_sent(onward, way, group, place, target)
                when_sent(jnp.logical_not(over_line(where)), 2, group, place, side)
                send(3, group, place, twin).start()

    lift = z == 0
    lower = z == depth - 1

    def side_arrival(step, group, k):
        if isinstance(step, int):
            place = side * pieces + k
            arrived(group, place)
            when_sent(lift, 0, group, place, up)
            when_sent(lower, 1, group, place, down)
            send(3, group, place, twin).start()
            return
        for sign in (-1, 1):
            where = z + sign * step

            @pl.when((where >= 0) & (where < depth))
            def _():
                place = slot(where, 1 - x, c) * pieces + k
                arrived(group, place)
                send(3, group, place, twin).start()

    order = [(t + d) % groups for d in range(groups)]

    def early(j):
        if j == 1:
            for group in order[1:]:
                arrived(group, me * pieces)
                first_spread(group, 0)
        if j == 2:
            column_arrival(1, order[0], 0)
        if j == 3:
            side_arrival(0, order[0], 0)
            for group in order[1:]:
                column_arrival(1, group, 0)

    fetch_table.wait()
    for k in range(pieces):
        for j in range(rows // batch):
            i = k * (rows // batch) + j
            load(i).wait()
            block = stream[i % depth_in].reshape(batch * channels, records_ref.shape[2])
            both = lax.dot_general(
                table[...], block, (((1,), (1,)), ((), ())), preferred_element_type=jnp.float32
            )
            if i + depth_in < batches:
                load(i + depth_in).start()
            if k == 1:
                early(j)
            for r in range(batch):
                real = both[:BINS, r * channels:(r + 1) * channels]
                imag = both[BINS:, r * channels:(r + 1) * channels]
                power = jnp.mean(real * real + imag * imag, axis=1, keepdims=True)
                inverse = 1.0 / jnp.sqrt(power + 1e-06)
                raw[j * batch + r, :BINS] = real * inverse
                raw[j * batch + r, BINS:] = imag * inverse
        turned = jnp.transpose(raw[...], (1, 0, 2)).astype(jnp.bfloat16)
        for h in range(groups):
            for part in range(2):
                for f in range(bins):
                    col = (part * bins + f) * channels
                    own[h, k, :, col:col + channels] = turned[part * BINS + h * bins + f]
        if k == 0:
            pl.semaphore_wait(
                barrier, groups + 1 + has_up.astype(jnp.int32) + has_down.astype(jnp.int32)
            )
            for d in range(1, groups):
                map_copy(d).start()
        for d in range(1, groups):
            tm_copy(d, k).start()
        first_spread(t, k, own.at[t, k])
        keep(k).start()

    fetch_blocks.wait()
    keep_map.wait()
    split = pieces > 1
    for k in range(1 if split else 0, pieces):
        for group in order[1:]:
            arrived(group, me * pieces + k)
            first_spread(group, k)
    for k in range(1 if split else 0, pieces):
        for group in order:
            column_arrival(1, group, k)
    for k in range(pieces):
        for group in order:
            if not (split and k == 0) or group is not order[0]:
                side_arrival(0, group, k)

    total = maps.shape[2]
    wanted_lane = lax.broadcasted_iota(jnp.int32, (WIN, total), 0) * NB
    lane = lax.broadcasted_iota(jnp.int32, (WIN, total), 1)
    column = lax.broadcasted_iota(jnp.int32, (WIN, layer), 1)
    for d, group in enumerate(order):
        if d:
            pltpu.make_async_copy(maps.at[group], maps.at[group], map_recv.at[group]).wait()
        row = jnp.broadcast_to(maps[group], (WIN, total))
        for ref in range(2 * slots):
            block = blocks[0, ref % 2:ref % 2 + 1, ref // 2:ref // 2 + 1]
            source = jnp.sum(
                jnp.where(lane == wanted_lane + block, row, 0), axis=1, keepdims=True
            )
            source = jnp.where(block >= 0, source, -1)
            for zz in range(depth):
                hit = (column + zz * layer == source).astype(jnp.float32).astype(jnp.bfloat16)
                onehot[group, zz, ref * WIN:(ref + 1) * WIN, :] = hit
    picked_ref[...] = jnp.zeros_like(picked_ref)
    for k in range(pieces):
        keep(k).wait()

    def pick(zz):
        for group in order:
            for xx in range(2):
                for k in range(pieces):
                    arrived(group, slot(zz, xx, 1 - c) * pieces + k)

        @pl.loop(0, groups)
        def _(group):
            rows_in = spectra[group, pl.ds(zz * 4 * pieces, 4 * pieces)].reshape(layer, width)
            found = jnp.dot(onehot[group, zz], rows_in, preferred_element_type=jnp.float32)
            picked_ref[group] += found.astype(jnp.bfloat16)

    @pl.loop(2, depth + 2)
    def _(step):
        for k in range(pieces):
            for group in order:
                column_arrival(step, group, k)
        for k in range(pieces):
            for group in order:
                side_arrival(step - 1, group, k)

        for sign in (1, -1):
            where = z + sign * (step - 2)
            there = (where >= 0) & (where < depth)

            @pl.when(there & (step > (1 if sign == 1 else 2)))
            def _():
                pick(where)

    for d in range(1, groups):
        map_copy(d).wait_send()
        for k in range(pieces):
            tm_copy(d, k).wait_send()

    for k in range(pieces):
        for group in order:
            @pl.when(lift)
            def _():
                send(0, group, side * pieces + k, up).wait_send()

            @pl.when(lower)
            def _():
                send(1, group, side * pieces + k, down).wait_send()

    @pl.loop(0, depth)
    def _(zz):
        for k in range(pieces):
            for group in order:
                place = slot(zz, x, c) * pieces + k

                @pl.when(has_up & (zz <= z))
                def _():
                    send(0, group, place, up).wait_send()

                @pl.when(has_down & (zz >= z))
                def _():
                    send(1, group, place, down).wait_send()

                @pl.when(jnp.logical_not(over_line(zz)))
                def _():
                    send(2, group, place, side).wait_send()

                send(3, group, place, twin).wait_send()
                send(3, group, slot(zz, 1 - x, c) * pieces + k, twin).wait_send()


def gather_picked(pair_blocks, source_map, table, records, groups, pairs):
    items, channels, length = records.shape
    slots = pair_blocks.shape[2]
    width = 2 * (BINS // groups) * channels
    rows = min(16, items)
    pieces = items // rows
    batch = min(4, rows)
    dtype = jnp.bfloat16
    vmem = pl.BlockSpec(memory_space=pltpu.VMEM)
    return pl.pallas_call(
        functools.partial(gather_kernel, groups, pairs),
        out_shape=jax.ShapeDtypeStruct((groups, 2 * slots * WIN, width), dtype),
        in_specs=[pl.BlockSpec(memory_space=pltpu.HBM)] * 4,
        out_specs=vmem,
        scratch_shapes=[
            pltpu.VMEM((2 * BINS, length), dtype),
            pltpu.VMEM(pair_blocks.shape, jnp.int32),
            pltpu.VMEM((3, batch, channels, length), dtype),
            pltpu.VMEM((rows, 2 * BINS, channels), jnp.float32),
            pltpu.VMEM((groups, pieces, rows, width), dtype),
            pltpu.VMEM((groups, pairs * pieces, rows, width), dtype),
            pltpu.VMEM((groups,) + source_map.shape, jnp.int32),
            pltpu.VMEM((groups, pairs // 4, 2 * slots * WIN, 4 * items), dtype),
            pltpu.SemaphoreType.DMA((3,)),
            pltpu.SemaphoreType.DMA((3,)),
            pltpu.SemaphoreType.DMA((4, groups, pairs * pieces)),
            pltpu.SemaphoreType.DMA((groups, pairs * pieces)),
            pltpu.SemaphoreType.DMA((groups, pieces)),
            pltpu.SemaphoreType.DMA((groups,)),
            pltpu.SemaphoreType.DMA((groups,)),
            pltpu.SemaphoreType.DMA((pieces,)),
        ],
        compiler_params=pltpu.CompilerParams(
            collective_id=0, has_side_effects=True, vmem_limit_bytes=63 << 20
        ),
        name="gather_picked",
    )(pair_blocks, source_map, table, records)


def stack_kernel(groups, scale, picked_ref, out_ref, done, sems):
    slots, bins, _, channels, _ = out_ref.shape

    def write(s, f):
        return pltpu.make_async_copy(done.at[s, f], out_ref.at[s, f], sems.at[s, f])

    for s in range(slots):
        left = slice(2 * s * WIN, (2 * s + 1) * WIN)
        right = slice((2 * s + 1) * WIN, (2 * s + 2) * WIN)
        for f in range(bins):
            real = slice(f * channels, (f + 1) * channels)
            imag = slice((bins + f) * channels, (bins + f + 1) * channels)
            x_re = [picked_ref[g, left, real] for g in range(groups)]
            x_im = [picked_ref[g, left, imag] for g in range(groups)]
            y_re = jnp.concatenate([picked_ref[g, right, real] for g in range(groups)], axis=0)
            y_im = jnp.concatenate([picked_ref[g, right, imag] for g in range(groups)], axis=0)
            lhs = jnp.concatenate(x_re + x_im, axis=0)
            rhs = jnp.concatenate(
                [
                    jnp.concatenate([y_re, -y_im], axis=1),
                    jnp.concatenate([y_im, y_re], axis=1),
                ],
                axis=0,
            )
            both = lax.dot_general(
                lhs, rhs, (((0,), (0,)), ((), ())), preferred_element_type=jnp.float32
            )
            done[s, f, 0] = both[:, :channels] * scale
            done[s, f, 1] = both[:, channels:] * scale
            write(s, f).start()
    for s in range(slots):
        for f in range(bins):
            write(s, f).wait()


def stack_pairs(slots, picked, channels):
    groups, _, width = picked.shape
    bins = width // (2 * channels)
    scale = 1.0 / math.sqrt(WIN * groups)
    vmem = pl.BlockSpec(memory_space=pltpu.VMEM)
    shape = (slots, bins, 2, channels, channels)
    return pl.pallas_call(
        functools.partial(stack_kernel, groups, scale),
        out_shape=jax.ShapeDtypeStruct(shape, jnp.float32),
        in_specs=[vmem],
        out_specs=pl.BlockSpec(memory_space=pl.ANY),
        scratch_shapes=[pltpu.VMEM(shape, jnp.float32), pltpu.SemaphoreType.DMA((slots, bins))],
        compiler_params=pltpu.CompilerParams(vmem_limit_bytes=40 << 20),
        name="stack_pairs",
    )(picked)


def per_device(groups, pairs, records, source_map, pair_blocks):
    table = jnp.asarray(transform_table(records.shape[3]))
    blocks = pair_blocks.transpose(0, 2, 1)
    picked = gather_picked(blocks, source_map, table, records[0], groups, pairs)
    return stack_pairs(pair_blocks.shape[1], picked, records.shape[2])


def solution(mesh):
    groups, pairs = mesh.shape["tm"], mesh.shape["pairs"]
    return jax.shard_map(
        functools.partial(per_device, groups, pairs),
        mesh=mesh,
        in_specs=(P("tm", "pairs", None, None), P("tm", None), P("pairs", None, None)),
        out_specs=P("pairs", "tm", None, None, None),
        check_vma=False,
    )
```

```python
import functools
import math

import jax
import jax.numpy as jnp
import numpy as np
from jax import lax
from jax.experimental import pallas as pl
from jax.experimental.pallas import tpu as pltpu
from jax.sharding import PartitionSpec as P

NB = 32
BINS = 16
FIRST_BIN = 64
WIN = 16
MESH = pl.DeviceIdType.MESH


def transform_table(length):
    samples = np.arange(length)
    phases = samples[None, :] * (FIRST_BIN + np.arange(BINS))[:, None] % length
    angles = 2.0 * np.pi / length * phases
    weight = (0.5 - 0.5 * np.cos(2.0 * np.pi / length * samples)) / math.sqrt(length)
    rows = np.concatenate([np.cos(angles) * weight, -np.sin(angles) * weight])
    return rows.astype(np.float32).astype(jnp.bfloat16)


def gather_kernel(groups, pairs, blocks_ref, map_ref, table_ref, records_ref, picked_ref,
                  stream, raw, own, spectra, maps, onehot,
                  load_sems, send_sems, recv_sems, tm_send, map_send, map_recv, keep_sems):
    items, channels, _ = records_ref.shape
    pieces, rows, width = own.shape[1:]
    batch = stream.shape[1]
    bins = width // (2 * channels)
    slots = blocks_ref.shape[1]
    depth = pairs // 4
    layer = 4 * items
    t = lax.axis_index("tm")
    me = lax.axis_index("pairs")
    z = me // 4
    x = (me // 2) % 2
    c = me % 2

    def slot(zz, xx, cc):
        return zz * 4 + xx * 2 + cc

    up, down = me + 4, me - 4
    side = slot(z, 1 - x, c)
    twin = slot(z, x, 1 - c)
    has_up = z < depth - 1
    has_down = z > 0
    batches = items // batch
    depth_in = stream.shape[0]

    def load(i):
        return pltpu.make_async_copy(
            records_ref.at[pl.ds(i * batch, batch)], stream.at[i % depth_in], load_sems.at[i % depth_in]
        )

    for i in range(min(depth_in, batches)):
        load(i).start()

    barrier = pltpu.get_barrier_semaphore()
    for d in range(1, groups):
        pl.semaphore_signal(barrier, inc=1, device_id=((t + d) % groups, me), device_id_type=MESH)
    for other in (side, twin):
        pl.semaphore_signal(barrier, inc=1, device_id=(t, other), device_id_type=MESH)

    @pl.when(has_up)
    def _():
        pl.semaphore_signal(barrier, inc=1, device_id=(t, up), device_id_type=MESH)

    @pl.when(has_down)
    def _():
        pl.semaphore_signal(barrier, inc=1, device_id=(t, down), device_id_type=MESH)

    def send(way, group, place, target, source=None):
        piece = spectra.at[group, place]
        return pltpu.make_async_remote_copy(
            src_ref=piece if source is None else source,
            dst_ref=piece,
            send_sem=send_sems.at[way, group, place],
            recv_sem=recv_sems.at[group, place],
            device_id=(t, target),
            device_id_type=MESH,
        )

    def arrived(group, place):
        pltpu.make_async_copy(
            spectra.at[group, place], spectra.at[group, place], recv_sems.at[group, place]
        ).wait()

    def tm_copy(d, k):
        peer = (t + d) % groups
        place = me * pieces + k
        return pltpu.make_async_remote_copy(
            src_ref=own.at[peer, k],
            dst_ref=spectra.at[t, place],
            send_sem=tm_send.at[d, k],
            recv_sem=recv_sems.at[t, place],
            device_id=(peer, me),
            device_id_type=MESH,
        )

    def map_copy(d):
        peer = (t + d) % groups
        return pltpu.make_async_remote_copy(
            src_ref=map_ref,
            dst_ref=maps.at[t],
            send_sem=map_send.at[d],
            recv_sem=map_recv.at[t],
            device_id=(peer, me),
            device_id_type=MESH,
        )

    def keep(k):
        return pltpu.make_async_copy(own.at[t, k], spectra.at[t, me * pieces + k], keep_sems.at[k])

    def spread(group, place, source, upward, downward):
        if upward is not None:
            @pl.when(upward)
            def _():
                send(0, group, place, up, source).start()
        if downward is not None:
            @pl.when(downward)
            def _():
                send(1, group, place, down, source).start()
        send(2, group, place, side, source).start()
        send(3, group, place, twin, source).start()

    order = [(t + d) % groups for d in range(groups)]

    for k in range(pieces):
        for j in range(rows // batch):
            i = k * (rows // batch) + j
            load(i).wait()
            block = stream[i % depth_in].reshape(batch * channels, records_ref.shape[2])
            both = lax.dot_general(
                table_ref[...], block, (((1,), (1,)), ((), ())), preferred_element_type=jnp.float32
            )
            if i + depth_in < batches:
                load(i + depth_in).start()
            for r in range(batch):
                real = both[:BINS, r * channels:(r + 1) * channels]
                imag = both[BINS:, r * channels:(r + 1) * channels]
                power = jnp.mean(real * real + imag * imag, axis=1, keepdims=True)
                inverse = 1.0 / jnp.sqrt(power + 1e-06)
                raw[j * batch + r, :BINS] = real * inverse
                raw[j * batch + r, BINS:] = imag * inverse
        turned = jnp.transpose(raw[...], (1, 0, 2)).astype(jnp.bfloat16)
        for h in range(groups):
            for part in range(2):
                for f in range(bins):
                    col = (part * bins + f) * channels
                    own[h, k, :, col:col + channels] = turned[part * BINS + h * bins + f]
        if k == 0:
            pl.semaphore_wait(
                barrier, groups + 1 + has_up.astype(jnp.int32) + has_down.astype(jnp.int32)
            )
            for d in range(1, groups):
                map_copy(d).start()
        spread(t, me * pieces + k, own.at[t, k], has_up, has_down)
        for d in range(1, groups):
            tm_copy(d, k).start()
        keep(k).start()

    maps[t] = map_ref[...]
    for k in range(pieces):
        for group in order[1:]:
            arrived(group, me * pieces + k)
            spread(group, me * pieces + k, None, has_up, has_down)

    total = maps.shape[2]
    wanted_lane = lax.broadcasted_iota(jnp.int32, (WIN, total), 0) * NB
    lane = lax.broadcasted_iota(jnp.int32, (WIN, total), 1)
    column = lax.broadcasted_iota(jnp.int32, (WIN, layer), 1)
    for d, group in enumerate(order):
        if d:
            pltpu.make_async_copy(maps.at[group], maps.at[group], map_recv.at[group]).wait()
        table = jnp.broadcast_to(maps[group], (WIN, total))
        for ref in range(2 * slots):
            block = blocks_ref[0, ref // 2, ref % 2]
            source = jnp.sum(
                jnp.where(lane == wanted_lane + block, table, 0), axis=1, keepdims=True
            )
            source = jnp.where(block >= 0, source, -1)
            for zz in range(depth):
                hit = (column + zz * layer == source).astype(jnp.float32).astype(jnp.bfloat16)
                onehot[group, zz, ref * WIN:(ref + 1) * WIN, :] = hit
    picked_ref[...] = jnp.zeros_like(picked_ref)
    for k in range(pieces):
        keep(k).wait()

    def pick(zz):
        for group in order:
            for xx in range(2):
                for k in range(pieces):
                    arrived(group, slot(zz, xx, 1 - c) * pieces + k)

        @pl.loop(0, groups)
        def _(group):
            rows_in = spectra[group, pl.ds(zz * 4 * pieces, 4 * pieces)].reshape(layer, width)
            found = jnp.dot(onehot[group, zz], rows_in, preferred_element_type=jnp.float32)
            picked_ref[group] += found.astype(jnp.bfloat16)

    @pl.loop(1, depth + 2)
    def _(step):
        for k in range(pieces):
            for group in order:
                @pl.when(z - step >= 0)
                def _():
                    place = slot(z - step, x, c) * pieces + k
                    arrived(group, place)
                    spread(group, place, None, has_up, None)

                @pl.when(z + step < depth)
                def _():
                    place = slot(z + step, x, c) * pieces + k
                    arrived(group, place)
                    spread(group, place, None, None, has_down)

        for k in range(pieces):
            for group in order:
                for sign in (1, -1):
                    where = z + sign * (step - 1)
                    there = (where >= 0) & (where < depth)

                    @pl.when(there if sign == 1 else there & (step > 1))
                    def _():
                        place = slot(where, 1 - x, c) * pieces + k
                        arrived(group, place)
                        send(3, group, place, twin).start()

        for sign in (1, -1):
            where = z + sign * (step - 2)
            there = (where >= 0) & (where < depth)

            @pl.when(there & (step > (1 if sign == 1 else 2)))
            def _():
                pick(where)

    for d in range(1, groups):
        map_copy(d).wait_send()
        for k in range(pieces):
            tm_copy(d, k).wait_send()

    @pl.loop(0, depth)
    def _(zz):
        for k in range(pieces):
            for group in order:
                place = slot(zz, x, c) * pieces + k

                @pl.when(has_up & (zz <= z))
                def _():
                    send(0, group, place, up).wait_send()

                @pl.when(has_down & (zz >= z))
                def _():
                    send(1, group, place, down).wait_send()

                send(2, group, place, side).wait_send()
                send(3, group, place, twin).wait_send()
                send(3, group, slot(zz, 1 - x, c) * pieces + k, twin).wait_send()


def gather_picked(pair_blocks, source_map, table, records, groups, pairs):
    items, channels, length = records.shape
    slots = pair_blocks.shape[1]
    width = 2 * (BINS // groups) * channels
    rows = min(16, items)
    pieces = items // rows
    batch = min(4, rows)
    dtype = jnp.bfloat16
    vmem = pl.BlockSpec(memory_space=pltpu.VMEM)
    return pl.pallas_call(
        functools.partial(gather_kernel, groups, pairs),
        out_shape=jax.ShapeDtypeStruct((groups, 2 * slots * WIN, width), dtype),
        in_specs=[
            pl.BlockSpec(memory_space=pltpu.SMEM),
            vmem,
            vmem,
            pl.BlockSpec(memory_space=pl.ANY),
        ],
        out_specs=vmem,
        scratch_shapes=[
            pltpu.VMEM((3, batch, channels, length), dtype),
            pltpu.VMEM((rows, 2 * BINS, channels), jnp.float32),
            pltpu.VMEM((groups, pieces, rows, width), dtype),
            pltpu.VMEM((groups, pairs * pieces, rows, width), dtype),
            pltpu.VMEM((groups,) + source_map.shape, jnp.int32),
            pltpu.VMEM((groups, pairs // 4, 2 * slots * WIN, 4 * items), dtype),
            pltpu.SemaphoreType.DMA((3,)),
            pltpu.SemaphoreType.DMA((4, groups, pairs * pieces)),
            pltpu.SemaphoreType.DMA((groups, pairs * pieces)),
            pltpu.SemaphoreType.DMA((groups, pieces)),
            pltpu.SemaphoreType.DMA((groups,)),
            pltpu.SemaphoreType.DMA((groups,)),
            pltpu.SemaphoreType.DMA((pieces,)),
        ],
        compiler_params=pltpu.CompilerParams(
            collective_id=0, has_side_effects=True, vmem_limit_bytes=40 << 20
        ),
        name="gather_picked",
    )(pair_blocks, source_map, table, records)


def stack_kernel(groups, scale, picked_ref, out_ref, done, sems):
    slots, bins, _, channels, _ = out_ref.shape

    def write(s, f):
        return pltpu.make_async_copy(done.at[s, f], out_ref.at[s, f], sems.at[s, f])

    for s in range(slots):
        left = slice(2 * s * WIN, (2 * s + 1) * WIN)
        right = slice((2 * s + 1) * WIN, (2 * s + 2) * WIN)
        for f in range(bins):
            real = slice(f * channels, (f + 1) * channels)
            imag = slice((bins + f) * channels, (bins + f + 1) * channels)
            x_re = [picked_ref[g, left, real] for g in range(groups)]
            x_im = [picked_ref[g, left, imag] for g in range(groups)]
            y_re = jnp.concatenate([picked_ref[g, right, real] for g in range(groups)], axis=0)
            y_im = jnp.concatenate([picked_ref[g, right, imag] for g in range(groups)], axis=0)
            lhs = jnp.concatenate(x_re + x_im, axis=0)
            rhs = jnp.concatenate(
                [
                    jnp.concatenate([y_re, -y_im], axis=1),
                    jnp.concatenate([y_im, y_re], axis=1),
                ],
                axis=0,
            )
            both = lax.dot_general(
                lhs, rhs, (((0,), (0,)), ((), ())), preferred_element_type=jnp.float32
            )
            done[s, f, 0] = both[:, :channels] * scale
            done[s, f, 1] = both[:, channels:] * scale
            write(s, f).start()
    for s in range(slots):
        for f in range(bins):
            write(s, f).wait()


def stack_pairs(slots, picked, channels):
    groups, _, width = picked.shape
    bins = width // (2 * channels)
    scale = 1.0 / math.sqrt(WIN * groups)
    vmem = pl.BlockSpec(memory_space=pltpu.VMEM)
    shape = (slots, bins, 2, channels, channels)
    return pl.pallas_call(
        functools.partial(stack_kernel, groups, scale),
        out_shape=jax.ShapeDtypeStruct(shape, jnp.float32),
        in_specs=[vmem],
        out_specs=pl.BlockSpec(memory_space=pl.ANY),
        scratch_shapes=[pltpu.VMEM(shape, jnp.float32), pltpu.SemaphoreType.DMA((slots, bins))],
        compiler_params=pltpu.CompilerParams(vmem_limit_bytes=40 << 20),
        name="stack_pairs",
    )(picked)


def per_device(groups, pairs, records, source_map, pair_blocks):
    table = jnp.asarray(transform_table(records.shape[3]))
    picked = gather_picked(pair_blocks, source_map, table, records[0], groups, pairs)
    return stack_pairs(pair_blocks.shape[1], picked, records.shape[2])


def solution(mesh):
    groups, pairs = mesh.shape["tm"], mesh.shape["pairs"]
    return jax.shard_map(
        functools.partial(per_device, groups, pairs),
        mesh=mesh,
        in_specs=(P("tm", "pairs", None, None), P("tm", None), P("pairs", None, None)),
        out_specs=P("pairs", "tm", None, None, None),
        check_vma=False,
    )
```
